128 devices in a mesh: dp: 16 (over x, z_lo, core), tensor: 8 (over z_hi, y).
Axes of the slice: x: 4, y: 4, z: 4 (z_hi: 2, z_lo: 2; z = z_hi * 2 + z_lo), core: 2. Of those that a mesh axis runs over, the one named last changes fastest.
Arguments:
- tokens: bfloat16 [8192, 4096], P('dp'), may hold values from -6 to 6
- gate_pre: bfloat16 [8192, 15360], P('dp', 'tensor'), may hold values from -6 to 6
- gated_cot: bfloat16 [8192, 15360], P('dp', 'tensor'), may hold values from -6 to 6
- gate_weight: bfloat16 [4096, 15360], P(None, 'tensor'), may hold values from -0.09375 to 0.09375
Outputs:
- input_grad: bfloat16 [8192, 4096], P('dp')
- gate_grad: float32 [4096, 15360], P('dp', 'tensor')
The draws below stay inside these ranges and needn't reach their ends.
All inputs are finite; a program needn't handle non-finite values.
Results may differ from the reference program's by a relative error of at most 0.0049.
Values may be sent and summed in bfloat16 or wider, within the bound.
No kernel may reach another device: no remote copies, remote signals or barrier semaphores. Data moves between devices by JAX's collectives and lax.ppermute only.
A program may use at most 192 MiB of HBM per device.

```python
import math
import jax
import jax.numpy as jnp
from jax import lax

DW = 4096
FFW = 15360
TOKENS = 8192


def with_spikes(array, key, source, target, blocks, factor):
    owner, partner = [(jnp.arange(array.shape[position]) // (array.shape[position] // blocks)).reshape([-1 if axis == position else 1 for axis in range(array.ndim)]) for position in (source, target)]
    chosen = jax.random.permutation(key, blocks)[partner]
    strong = (owner == chosen) | (owner == (partner + blocks // 2) % blocks)
    return jnp.where(strong, factor * array, array)


def shard_levels(rng, shape, pieces, least, top_value):
    def one(dim, blocks):
        heights = jax.random.uniform(jax.random.fold_in(jax.random.fold_in(rng, 6), dim), (blocks,), jnp.float32, least / len(pieces), top_value / len(pieces))
        return jnp.repeat(jnp.exp(heights), shape[dim] // blocks).reshape((-1,) + (1,) * (len(shape) - dim - 1))

    factor_of = one(*pieces[0])
    for cut in pieces[1:]:
        factor_of = factor_of * one(*cut)
    return factor_of


def gaussian(key, extent, deviation, reach, split=(), dtype=jnp.bfloat16):
    entries = jax.random.normal(key, extent, jnp.float32) * deviation
    if len(split) > 0:
        entries = shard_levels(key, extent, split, -0.22, 0.18) * entries
    return jnp.clip(entries, min=-reach, max=reach).astype(dtype)


def noise_with(key, extent, width, bound, cuts, heavy, dtype=jnp.bfloat16):
    drawn = width * jax.random.normal(key, extent, jnp.float32)
    if cuts:
        drawn = drawn * shard_levels(key, extent, cuts, -0.22, 0.18)
    return jnp.clip(with_spikes(drawn, jax.random.fold_in(key, 3), *heavy), -bound, bound).astype(dtype)


def setup_inputs(seed: int = 0) -> dict:
    seeds = jax.random.split(jax.random.key(seed), 5)
    return {
        "tokens": noise_with(seeds[0], (TOKENS, DW), 1.0, 6.0, ((0, 16),), (0, 1, 16, 2.0)),
        "gate_pre": gaussian(seeds[1], (TOKENS, FFW), 1.0, 6.0, ((0, 16), (1, 8))),
        "gated_cot": gaussian(seeds[2], (TOKENS, FFW), 1.0, 6.0, ((0, 16), (1, 8))),
        "gate_weight": gaussian(seeds[3], (DW, FFW), DW ** -0.5, 0.09375, ((1, 8),)),
    }


def reference(tokens, gate_pre, gated_cot, gate_weight):
    gate_val = gate_pre.astype(jnp.float32)
    cot_val = gated_cot.astype(jnp.float32)
    sigmoid_val = 1.0 / (1.0 + jnp.exp(-gate_val))
    gate_cot = (cot_val * sigmoid_val * (1.0 + gate_val * (1.0 - sigmoid_val))).astype(jnp.bfloat16)
    input_grad = lax.dot_general(gate_cot, gate_weight, (((1,), (1,)), ((), ())), preferred_element_type=jnp.float32).astype(jnp.bfloat16)
    factor = 1.0 / math.sqrt(TOKENS)
    gate_grad = lax.dot_general(tokens, gate_cot, (((0,), (0,)), ((), ())), preferred_element_type=jnp.float32) * factor
    return (input_grad, gate_grad)
```

```python
import math

import jax
import jax.numpy as jnp
from jax import lax
from jax.sharding import PartitionSpec as P

CORE_SWAP = [(d, d ^ 1) for d in range(16)]
ZLO_SWAP = [(d, d ^ 2) for d in range(16)]
ZHI_SWAP = [(t, t ^ 4) for t in range(8)]


def x_shift(step):
    return [(d, (d + 4 * step) % 16) for d in range(16)]


def y_shift(step):
    return [(t, t // 4 * 4 + (t + step) % 4) for t in range(8)]


def halves(rows):
    return (slice(0, rows // 2), slice(rows // 2, rows))


def ring_sums(part, axis, shift):
    right, left = shift(1), shift(-1)
    far_r = lax.ppermute(part(2, 0), axis, right)
    far_l = lax.ppermute(part(2, 1), axis, left)
    own_r = lax.ppermute(part(1, 1), axis, right)
    own_l = lax.ppermute(part(3, 0), axis, left)
    sum_r = lax.ppermute(part(1, 0, far_r), axis, right)
    sum_l = lax.ppermute(part(3, 1, far_l), axis, left)
    return ((sum_r, own_l), (own_r, sum_l))


def per_device(tokens, gate_pre, gated_cot, gate_weight):
    bf16, f32 = jnp.bfloat16, jnp.float32
    dp, tensor = lax.axis_index("dp"), lax.axis_index("tensor")
    x, zlo, core, y = dp // 4, dp // 2 % 2, dp % 2, tensor % 4
    n_tok, width = tokens.shape
    hidden = gate_pre.shape[1]
    block = width // 16

    def token_piece(step, half, of_core):
        owner = (x + step) % 4 * 4 + jnp.bitwise_xor(zlo, half) * 2 + of_core
        return lax.dynamic_slice(tokens, (0, owner * block), (n_tok, block))

    order = [(step, half) for step in (2, 1, 3, 0) for half in (0, 1)]
    theirs = jnp.stack([token_piece(s, h, 1 - core) for s, h in order])
    theirs = lax.ppermute(theirs, "dp", CORE_SWAP)
    pieces = {
        sh: jnp.concatenate([token_piece(*sh, core), theirs[i]], 0) for i, sh in enumerate(order)
    }

    gate_val = gate_pre.astype(f32)
    cot_val = gated_cot.astype(f32)
    sigmoid_val = 1.0 / (1.0 + jnp.exp(-gate_val))
    gate_cot = (cot_val * sigmoid_val * (1.0 + gate_val * (1.0 - sigmoid_val))).astype(bf16)
    gate_cot = lax.optimization_barrier(gate_cot)
    both_cot = jnp.concatenate([gate_cot, lax.ppermute(gate_cot, "dp", CORE_SWAP)], 0)

    rows = halves(n_tok)
    chunks = 2
    cols = width // 4 // chunks

    def input_part(chunk):
        def part(step, half, *received):
            start = ((y + step) % 4 * chunks + chunk) * cols
            weight = lax.dynamic_slice(gate_weight, (start, 0), (cols, hidden))
            value = lax.dot_general(
                gate_cot[rows[half]], weight, (((1,), (1,)), ((), ())), preferred_element_type=f32
            )
            for other in received:
                value = value + other.astype(f32)
            return value.astype(bf16)

        return part

    input_grad = jnp.zeros((n_tok, width), bf16)

    def put(out, value, step, chunk, row):
        start = ((y + step) % 4 * chunks + chunk) * cols
        return lax.dynamic_update_slice(out, value, (row, start))

    for chunk in range(chunks):
        part = input_part(chunk)
        left_over = ring_sums(part, "tensor", y_shift)
        mine = jnp.concatenate([part(0, half, *left_over[half]) for half in (0, 1)], 0)
        other = lax.ppermute(mine, "tensor", ZHI_SWAP)
        done = (mine.astype(f32) + other.astype(f32)).astype(bf16)
        from_l = lax.ppermute(done, "tensor", y_shift(1))
        from_r = lax.ppermute(done, "tensor", y_shift(-1))
        far_0 = lax.ppermute(from_l[rows[0]], "tensor", y_shift(1))
        far_1 = lax.ppermute(from_r[rows[1]], "tensor", y_shift(-1))
        input_grad = put(input_grad, done, 0, chunk, 0)
        input_grad = put(input_grad, from_l, 3, chunk, 0)
        input_grad = put(input_grad, from_r, 1, chunk, 0)
        input_grad = put(input_grad, far_0, 2, chunk, 0)
        input_grad = put(input_grad, far_1, 2, chunk, n_tok // 2)

    factor = 1.0 / math.sqrt(n_tok * lax.axis_size("dp"))

    def weight_part(columns):
        def exact(step, half, *received):
            value = lax.dot_general(
                pieces[step, half],
                both_cot[:, columns],
                (((0,), (0,)), ((), ())),
                preferred_element_type=f32,
            )
            for other in received:
                value = value + other.astype(f32)
            return value

        return exact

    grads = []
    for columns in (slice(0, 1024), slice(1024, hidden)):
        exact = weight_part(columns)
        left_over = ring_sums(lambda *a: exact(*a).astype(bf16), "dp", x_shift)
        other = lax.ppermute(exact(0, 1, *left_over[1]).astype(bf16), "dp", ZLO_SWAP)
        grads.append(exact(0, 0, *left_over[0], other) * factor)
    return (input_grad, jnp.concatenate(grads, 1))


def solution(mesh):
    placed = (P("dp", None), P("dp", "tensor"), P("dp", "tensor"), P(None, "tensor"))
    return jax.shard_map(
        per_device,
        mesh=mesh,
        in_specs=placed,
        out_specs=(P("dp", None), P("dp", "tensor")),
        check_vma=False,
    )
```

```python
import math

import jax
import jax.numpy as jnp
from jax import lax
from jax.experimental import pallas as pl
from jax.experimental.pallas import tpu as pltpu
from jax.sharding import PartitionSpec as P

CORE_SWAP = [(d, d ^ 1) for d in range(16)]
ZLO_SWAP = [(d, d ^ 2) for d in range(16)]
ZHI_SWAP = [(t, t ^ 4) for t in range(8)]


def over(i, which):
    return 3 - i if which else i ^ 1


X_SWAP = [[(d, over(d // 4, d % 2 ^ step) * 4 + d % 4) for d in range(16)] for step in range(2)]
Y_SWAP = [
    [(d * 8 + t, d * 8 + t // 4 * 4 + over(t % 4, d % 2 ^ step)) for d in range(16) for t in range(8)]
    for step in range(2)
]
BF16, F32 = jnp.bfloat16, jnp.float32
PARAMS = pltpu.CompilerParams(vmem_limit_bytes=20 * 2**20)
BLOCK = 256
QUARTER = 512
UNIT = 4 * QUARTER
COLS = ((0, 768), (768, 1536), (1536, 1920))
VMEM = pl.BlockSpec(memory_space=pltpu.VMEM)
SMEM = pl.BlockSpec(memory_space=pltpu.SMEM)
HBM = pl.BlockSpec(memory_space=pltpu.HBM)
QUICK = pl.CostEstimate(flops=0, transcendentals=0, bytes_accessed=0)
G_AT, T_AT = 0, 8


def g_at(half, d1, d2):
    return G_AT + (1 - d1) * 4 + d2 * 2 + half


def t_at(dh, dq):
    return T_AT + dh * 2 + dq


def pack_call(table, first, tok, their_tok, cots):
    n_tok = tok.shape[0]

    def body(table_ref, tok_ref, their_tok_ref, *refs):
        turned = refs[len(cots)]
        for n in range(4):
            here = pl.ds(pl.multiple_of(table_ref[G_AT + first + n] * BLOCK, BLOCK), BLOCK)
            turned[n, :, :n_tok] = tok_ref[:, here].T
            turned[n, :, n_tok:] = their_tok_ref[:, here].T
        for n in range(len(cots)):
            refs[-1][n * n_tok : (n + 1) * n_tok] = refs[n][...]

    shapes = [jax.ShapeDtypeStruct((4, BLOCK, 2 * n_tok), BF16)]
    if cots:
        shapes.append(jax.ShapeDtypeStruct((2 * n_tok, cots[0].shape[1]), BF16))
    return pl.pallas_call(
        body,
        in_specs=[SMEM] + [VMEM] * (2 + len(cots)),
        out_specs=[VMEM] * len(shapes),
        out_shape=shapes,
        compiler_params=PARAMS,
        cost_estimate=QUICK,
        name="pack",
    )(table, tok, their_tok, *cots)


def weight_call(table, data, jobs, cols, outs):
    flat = [a for _, adds in jobs for a in adds]
    lo, hi = cols

    def body(table_ref, *refs):
        n = len(data) - 1
        turned, both, refs = refs[:n], refs[n], refs[n + 1 :]
        added = iter(zip(refs, flat))
        out_refs = refs[len(flat) :]
        slots = [(o, i) for o, n in enumerate(outs) for i in range(n)]
        for (at, adds), (o, i) in zip(jobs, slots):
            value = jnp.dot(turned[at // 4][at % 4], both[:, lo:hi], preferred_element_type=F32)
            for _ in adds:
                ref, (_, index) = next(added)
                value += (ref[...] if index is None else ref[index]).astype(F32)
            if outs[o] == 1:
                out_refs[o][...] = value.astype(BF16)
            else:
                out_refs[o][i] = value.astype(BF16)

    return pl.pallas_call(
        body,
        in_specs=[SMEM] + [VMEM] * (len(data) + len(flat)),
        out_specs=[VMEM] * len(outs),
        out_shape=[
            jax.ShapeDtypeStruct((BLOCK, hi - lo) if n == 1 else (n, BLOCK, hi - lo), BF16) for n in outs
        ],
        compiler_params=PARAMS,
        cost_estimate=QUICK,
        name="weight_term",
    )(table, *data, *[a for a, _ in flat])


def final_call(table, turned, both, parts, factor, into):
    tile = 384
    hidden = both.shape[1]
    flat, tiles = [], []
    for (lo, hi), adds in parts:
        which = range(len(flat), len(flat) + len(adds))
        tiles += [(start, start - lo, which) for start in range(lo, hi, tile)]
        flat += adds

    def body(table_ref, turned_ref, both_ref, *refs):
        for j, (start, inner, which) in enumerate(tiles):

            @pl.when(pl.program_id(0) == j)
            def _():
                here = slice(inner, inner + tile)
                value = jnp.dot(turned_ref[0], both_ref[:, start : start + tile], preferred_element_type=F32)
                for k in which:
                    index = flat[k][1]
                    value += (refs[k][:, here] if index is None else refs[k][index, :, here]).astype(F32)
                refs[-1][...] = value * factor

    first = tiles[0][0] // tile
    return pl.pallas_call(
        body,
        grid=(len(tiles),),
        in_specs=[SMEM] + [VMEM] * (2 + len(flat)) + [pl.BlockSpec(memory_space=pl.ANY)] * (into is not None),
        out_specs=pl.BlockSpec((BLOCK, tile), lambda j: (0, first + j)),
        out_shape=jax.ShapeDtypeStruct((BLOCK, hidden), F32),
        input_output_aliases={} if into is None else {3 + len(flat): 0},
        compiler_params=PARAMS,
        cost_estimate=QUICK,
        name="weight_grad",
    )(table, turned, both, *[a for a, _ in flat], *([] if into is None else [into]))


def input_call(table, cot, weight, unit, jobs, n_out, fetch):
    flat = [a for _, adds in jobs for a in adds]
    n_tok, hidden = cot.shape
    half = QUARTER // 2

    def body(table_ref, cot_ref, w_ref, *refs):
        added = iter(zip(refs, flat))
        out = refs[len(flat)]

        def rows(at, part):
            start = unit * UNIT + table_ref[at] * QUARTER + part * half
            return pl.ds(pl.multiple_of(start, half), half)

        parts = [(k, part) for k in range(len(jobs)) for part in range(2)]
        copies = []
        if fetch:
            buf, sems = refs[len(flat) + 1 :]
            for n, (k, part) in enumerate(parts):
                copies.append(pltpu.make_async_copy(w_ref.at[rows(jobs[k][0], part)], buf.at[n], sems.at[n]))
            for copy in copies:
                copy.start()
        for n, (k, part) in enumerate(parts):
            if part == 0:
                extras = [next(added) for _ in jobs[k][1]]
            if fetch:
                copies[n].wait()
            w = buf[n] if fetch else w_ref[rows(jobs[k][0], part)]
            value = lax.dot_general(cot_ref[...], w, (((1,), (1,)), ((), ())), preferred_element_type=F32)
            here = slice(part * half, (part + 1) * half)
            for ref, (_, index) in extras:
                value += (ref[:, here] if index is None else ref[index, :, here]).astype(F32)
            if n_out == 1:
                out[:, here] = value.astype(BF16)
            else:
                out[k, :, here] = value.astype(BF16)

    n = 2 * len(jobs)
    scratch = [pltpu.VMEM((n, half, hidden), BF16), pltpu.SemaphoreType.DMA((n,))] if fetch else []
    if fetch:
        weight = pltpu.with_memory_space_constraint(weight, pltpu.HBM)
    return pl.pallas_call(
        body,
        in_specs=[SMEM, VMEM, HBM if fetch else VMEM] + [VMEM] * len(flat),
        out_specs=VMEM,
        out_shape=jax.ShapeDtypeStruct((n_tok, QUARTER) if n_out == 1 else (n_out, n_tok, QUARTER), BF16),
        scratch_shapes=scratch,
        compiler_params=PARAMS,
        cost_estimate=QUICK,
        name="input_term",
    )(table, cot, weight, *[a for a, _ in flat])


def sum_call(table, mine, other):
    def body(table_ref, a, b, out):
        out[...] = (a[...].astype(F32) + b[...].astype(F32)).astype(BF16)

    return pl.pallas_call(
        body,
        in_specs=[SMEM, VMEM, VMEM],
        out_specs=VMEM,
        out_shape=jax.ShapeDtypeStruct(mine.shape, BF16),
        compiler_params=PARAMS,
        cost_estimate=QUICK,
        name="input_sum",
    )(table, mine, other)


def pair_call(table, a, b):
    def body(table_ref, a_ref, b_ref, out):
        out[0] = a_ref[...]
        out[1] = b_ref[...]

    return pl.pallas_call(
        body,
        in_specs=[SMEM, VMEM, VMEM],
        out_specs=VMEM,
        out_shape=jax.ShapeDtypeStruct((2, *a.shape), BF16),
        compiler_params=PARAMS,
        cost_estimate=QUICK,
        name="input_pair",
    )(table, a, b)


def put_call(table, out, width, unit, halves):
    n_tok = halves[0].shape[1]

    def body(table_ref, *refs):
        for dh in range(2):
            for dq in range(2):
                start = pl.multiple_of(table_ref[t_at(dh, dq)] * QUARTER, QUARTER)
                refs[-1][:, pl.ds(start, QUARTER)] = refs[dh][dq]

    return pl.pallas_call(
        body,
        grid=(1,),
        in_specs=[SMEM, VMEM, VMEM] + [pl.BlockSpec(memory_space=pl.ANY)] * (out is not None),
        out_specs=pl.BlockSpec((n_tok, UNIT), lambda j: (0, unit)),
        out_shape=jax.ShapeDtypeStruct((n_tok, width), BF16),
        input_output_aliases={} if out is None else {3: 0},
        compiler_params=PARAMS,
        cost_estimate=QUICK,
        name="place_columns",
    )(table, *halves, *([] if out is None else [out]))


def per_device(tokens, gate_pre, gated_cot, gate_weight):
    dp, tensor = lax.axis_index("dp"), lax.axis_index("tensor")
    x, zlo, core, y = dp // 4, dp // 2 % 2, dp % 2, tensor % 4
    n_tok, width = tokens.shape
    hidden = gate_pre.shape[1]

    def bits(i):
        return (i + 1) // 2 % 2, i // 2

    xor = jnp.bitwise_xor

    def in_order(first, second):
        return jnp.where(core == 0, first, second), jnp.where(core == 0, second, first)

    (ux, vx), (h, q) = bits(x), in_order(*bits(y))
    entries = []
    for d1 in (1, 0):
        for d2 in range(2):
            for half in range(2):
                du, dv = in_order(d1, d2)
                owner = xor(xor(ux, du), 3 * xor(vx, dv))
                entries.append(owner * 4 + xor(zlo, half) * 2 + core)
    entries += [xor(h, dh) * 2 + xor(q, dq) for dh in range(2) for dq in range(2)]
    table = jnp.stack(entries).astype(jnp.int32)

    last = [table]

    def ordered():
        return lax.optimization_barrier((table, last[0]))[0]

    their_tok = lax.ppermute(tokens, "dp", CORE_SWAP)
    gate_val = gate_pre.astype(F32)
    cot_val = gated_cot.astype(F32)
    sigmoid_val = 1.0 / (1.0 + jnp.exp(-gate_val))
    gate_cot = (cot_val * sigmoid_val * (1.0 + gate_val * (1.0 - sigmoid_val))).astype(BF16)
    their_cot = lax.ppermute(gate_cot, "dp", CORE_SWAP)

    def t_call(*args, **more):
        last[0] = input_call(ordered(), gate_cot, gate_weight, *args, **more)
        return last[0]

    def g_call(*args):
        last[0] = weight_call(ordered(), [d for d in data if d is not None], *args)[0]
        return last[0]

    def y_swap(value, step):
        return lax.ppermute(value, ("dp", "tensor"), Y_SWAP[step])

    def x_swap(value, step):
        return lax.ppermute(value, "dp", X_SWAP[step])

    def z_swap(value):
        return lax.ppermute(value, "dp", ZLO_SWAP)

    class Unit:
        def __init__(self, unit):
            self.unit = unit

    def t_first(g, fetch):
        g.one = y_swap(t_call(g.unit, [(t_at(1, 0), []), (t_at(1, 1), [])], 2, fetch), 0)

    def t_second(g):
        g.two = y_swap(t_call(g.unit, [(t_at(0, 1), [(g.one, 1)])], 1, False), 1)

    def t_third(g):
        g.mine = t_call(g.unit, [(t_at(0, 0), [(g.one, 0), (g.two, None)])], 1, False)
        g.other = lax.ppermute(g.mine, "tensor", ZHI_SWAP)

    def t_fourth(g):
        last[0] = g.done = sum_call(ordered(), g.mine, g.other)
        g.near = y_swap(g.done, 1)

    def t_fifth(g):
        last[0] = g.half = pair_call(ordered(), g.done, g.near)
        g.far = y_swap(g.half, 0)

    def t_sixth(g, out):
        last[0] = put_call(ordered(), out, width, g.unit, (g.half, g.far))
        return last[0]

    class Part:
        def __init__(self, cols):
            self.cols = cols

    def g_first(g):
        jobs = [(g_at(half, 1, d2), []) for d2 in range(2) for half in range(2)]
        g.one = x_swap(g_call(jobs, g.cols, [4]), 0)

    def g_second(g):
        jobs = [(g_at(half, 0, 1), [(g.one, 2 + half)]) for half in range(2)]
        g.two = x_swap(g_call(jobs, g.cols, [2]), 1)

    def g_third(g):
        g.other = z_swap(g_call([(g_at(1, 0, 0), [(g.one, 1), (g.two, 1)])], g.cols, [1]))
        g.adds = [(g.one, 0), (g.two, 0), (g.other, None)]

    factor = 1.0 / math.sqrt(n_tok * lax.axis_size("dp"))

    def g_final(parts, grad):
        last[0] = final_call(ordered(), data[1], data[2], [(g.cols, g.adds) for g in parts], factor, grad)
        return last[0]

    a, b = Unit(0), Unit(1)
    k, l, m = (Part(cols) for cols in COLS)
    t_first(a, True)
    ahead, both = pack_call(ordered(), 0, tokens, their_tok, [gate_cot, their_cot])
    last[0] = ahead
    data = (ahead, None, both)
    g_first(k)
    t_first(b, False)
    last[0] = pack_call(ordered(), 4, tokens, their_tok, [])[0]
    data = (ahead, last[0], both)
    g_first(l)
    t_second(a)
    t_third(a)
    t_second(b)
    g_second(k)
    g_first(m)
    t_third(b)
    t_fourth(a)
    g_second(l)
    t_fifth(a)
    g_third(k)
    g_second(m)
    t_fourth(b)
    g_third(l)
    t_fifth(b)
    g_third(m)
    out = t_sixth(a, None)
    grad = g_final([k, l], None)
    grad = g_final([m], grad)
    out = t_sixth(b, out)
    return (out, grad)


def solution(mesh):
    placed = (P("dp", None), P("dp", "tensor"), P("dp", "tensor"), P(None, "tensor"))
    return jax.shard_map(
        per_device,
        mesh=mesh,
        in_specs=placed,
        out_specs=(P("dp", None), P("dp", "tensor")),
        check_vma=False,
    )
```

```python
import math

import jax
import jax.numpy as jnp
from jax import lax
from jax.experimental import pallas as pl
from jax.experimental.pallas import tpu as pltpu
from jax.sharding import PartitionSpec as P

CORE_SWAP = [(d, d ^ 1) for d in range(16)]
ZLO_SWAP = [(d, d ^ 2) for d in range(16)]
ZHI_SWAP = [(t, t ^ 4) for t in range(8)]


def over(i, which):
    return 3 - i if which else i ^ 1


X_SWAP = [[(d, over(d // 4, d % 2 ^ step) * 4 + d % 4) for d in range(16)] for step in range(2)]
Y_SWAP = [
    [(d * 8 + t, d * 8 + t // 4 * 4 + over(t % 4, d % 2 ^ step)) for d in range(16) for t in range(8)]
    for step in range(2)
]
BF16, F32 = jnp.bfloat16, jnp.float32
PARAMS = pltpu.CompilerParams(vmem_limit_bytes=12 * 2**20)
BLOCK = 256
QUARTER = 512
UNIT = 4 * QUARTER
FETCH = True
GATE_KERNEL = False
Z_FIRST = False
SLICE = True
COLS = ((0, 768), (768, 1536), (1536, 1920))
ORDER = "a1 P1 k1 b1 P2 l1 a2 b2 a3 k2 m1 b3 a4 l2 b4 a5 k3 l3 wa1 b5 m2 wl3 m3 wk1 b6 a7 kl4 m4 b7"
VMEM = pl.BlockSpec(memory_space=pltpu.VMEM)
SMEM = pl.BlockSpec(memory_space=pltpu.SMEM)
HBM = pl.BlockSpec(memory_space=pltpu.HBM)
QUICK = pl.CostEstimate(flops=0, transcendentals=0, bytes_accessed=0)
G_AT, T_AT = 0, 8


def g_at(half, d1, d2):
    return G_AT + (1 - d1) * 4 + d2 * 2 + half


def t_at(dh, dq):
    return T_AT + dh * 2 + dq


def gate_call(gate_pre, gated_cot):
    n_tok, hidden = gate_pre.shape
    rows = 64

    def body(pre_ref, cot_ref, out_ref):
        gate_val = pre_ref[...].astype(F32)
        cot_val = cot_ref[...].astype(F32)
        sigmoid_val = 1.0 / (1.0 + jnp.exp(-gate_val))
        out_ref[...] = (cot_val * sigmoid_val * (1.0 + gate_val * (1.0 - sigmoid_val))).astype(BF16)

    block = pl.BlockSpec((rows, hidden), lambda j: (j, 0))
    return pl.pallas_call(
        body,
        grid=(n_tok // rows,),
        in_specs=[block, block],
        out_specs=block,
        out_shape=jax.ShapeDtypeStruct((n_tok, hidden), BF16),
        compiler_params=PARAMS,
        cost_estimate=QUICK,
        name="gate_cot",
    )(gate_pre, gated_cot)


def pack_call(table, first, tok, their_tok, cots):
    n_tok = tok.shape[0]

    def body(table_ref, tok_ref, their_tok_ref, *refs):
        turned = refs[len(cots)]
        for n in range(4):
            here = pl.ds(pl.multiple_of(table_ref[G_AT + first + n] * BLOCK, BLOCK), BLOCK)
            turned[n, :, :n_tok] = tok_ref[:, here].T
            turned[n, :, n_tok:] = their_tok_ref[:, here].T
        for n in range(len(cots)):
            refs[-1][n * n_tok : (n + 1) * n_tok] = refs[n][...]

    shapes = [jax.ShapeDtypeStruct((4, BLOCK, 2 * n_tok), BF16)]
    if cots:
        shapes.append(jax.ShapeDtypeStruct((2 * n_tok, cots[0].shape[1]), BF16))
    return pl.pallas_call(
        body,
        in_specs=[SMEM] + [VMEM] * (2 + len(cots)),
        out_specs=[VMEM] * len(shapes),
        out_shape=shapes,
        compiler_params=PARAMS,
        cost_estimate=QUICK,
        name="pack",
    )(table, tok, pltpu.with_memory_space_constraint(their_tok, pltpu.VMEM), *cots)


def weight_call(table, data, jobs, cols, outs):
    flat = [a for _, adds in jobs for a in adds]
    lo, hi = cols

    def body(table_ref, *refs):
        n = len(data) - 1
        turned, both, refs = refs[:n], refs[n], refs[n + 1 :]
        added = iter(zip(refs, flat))
        out_refs = refs[len(flat) :]
        slots = [(o, i) for o, n in enumerate(outs) for i in range(n)]
        for (at, adds), (o, i) in zip(jobs, slots):
            value = jnp.dot(turned[at // 4][at % 4], both[:, lo:hi], preferred_element_type=F32)
            for _ in adds:
                ref, (_, index) = next(added)
                value += (ref[...] if index is None else ref[index]).astype(F32)
            if outs[o] == 1:
                out_refs[o][...] = value.astype(BF16)
            else:
                out_refs[o][i] = value.astype(BF16)

    return pl.pallas_call(
        body,
        in_specs=[SMEM] + [VMEM] * (len(data) + len(flat)),
        out_specs=[VMEM] * len(outs),
        out_shape=[
            jax.ShapeDtypeStruct((BLOCK, hi - lo) if n == 1 else (n, BLOCK, hi - lo), BF16) for n in outs
        ],
        compiler_params=PARAMS,
        cost_estimate=QUICK,
        name="weight_term",
    )(table, *data, *[a for a, _ in flat])


def final_call(table, turned, both, parts, factor, into):
    tile = parts[0][0][1] - parts[0][0][0]
    hidden = both.shape[1]
    flat, tiles = [], []
    for (lo, hi), adds in parts:
        which = range(len(flat), len(flat) + len(adds))
        tiles += [(start, start - lo, which) for start in range(lo, hi, tile)]
        flat += adds

    def body(table_ref, turned_ref, both_ref, *refs):
        for j, (start, inner, which) in enumerate(tiles):

            @pl.when(pl.program_id(0) == j)
            def _():
                here = slice(inner, inner + tile)
                value = jnp.dot(turned_ref[0], both_ref[:, start : start + tile], preferred_element_type=F32)
                for k in which:
                    index = flat[k][1]
                    value += (refs[k][:, here] if index is None else refs[k][index, :, here]).astype(F32)
                refs[-1][...] = value * factor

    first = tiles[0][0] // tile
    return pl.pallas_call(
        body,
        grid=(len(tiles),),
        in_specs=[SMEM] + [VMEM] * (2 + len(flat)) + [pl.BlockSpec(memory_space=pl.ANY)] * (into is not None),
        out_specs=pl.BlockSpec((BLOCK, tile), lambda j: (0, first + j)),
        out_shape=jax.ShapeDtypeStruct((BLOCK, hidden), F32),
        input_output_aliases={} if into is None else {3 + len(flat): 0},
        compiler_params=PARAMS,
        cost_estimate=QUICK,
        name="weight_grad",
    )(table, turned, both, *[a for a, _ in flat], *([] if into is None else [into]))


def input_call(table, cot, weight, unit, jobs, n_out, fetch, bring=None, local=False):
    flat = [a for _, adds in jobs for a in adds]
    n_tok, hidden = cot.shape
    half = QUARTER // 2

    def body(table_ref, cot_ref, w_ref, *refs):
        added = iter(zip(refs, flat))
        refs = refs[len(flat) :]
        if bring is not None:
            brought = pltpu.make_async_copy(refs[0], refs[2], refs[-1])
            out, refs = refs[1], refs[3:-1]
        else:
            out, refs = refs[0], refs[1:]

        def rows(at, part):
            start = (table_ref[at] % 2 if local else unit * (UNIT // QUARTER) + table_ref[at]) * QUARTER + part * half
            return pl.ds(pl.multiple_of(start, half), half)

        parts = [(k, part) for k in range(len(jobs)) for part in range(2)]
        copies = []
        if fetch:
            buf, sems = refs
            for n, (k, part) in enumerate(parts):
                copies.append(pltpu.make_async_copy(w_ref.at[rows(jobs[k][0], part)], buf.at[n], sems.at[n]))
            for copy in copies:
                copy.start()
        if bring is not None:
            brought.start()
        for n, (k, part) in enumerate(parts):
            if part == 0:
                extras = [next(added) for _ in jobs[k][1]]
            if fetch:
                copies[n].wait()
            w = buf[n] if fetch else w_ref[rows(jobs[k][0], part)]
            value = lax.dot_general(cot_ref[...], w, (((1,), (1,)), ((), ())), preferred_element_type=F32)
            here = slice(part * half, (part + 1) * half)
            for ref, (_, index) in extras:
                value += (ref[:, here] if index is None else ref[index, :, here]).astype(F32)
            if n_out == 1:
                out[:, here] = value.astype(BF16)
            else:
                out[k, :, here] = value.astype(BF16)
        if bring is not None:
            brought.wait()

    n = 2 * len(jobs)
    scratch = [pltpu.VMEM((n, half, hidden), BF16), pltpu.SemaphoreType.DMA((n,))] if fetch else []
    operands = [table, cot, weight, *[a for a, _ in flat]]
    in_specs = [SMEM, VMEM, HBM if fetch else VMEM] + [VMEM] * len(flat)
    out_shape = [jax.ShapeDtypeStruct((n_tok, QUARTER) if n_out == 1 else (n_out, n_tok, QUARTER), BF16)]
    if fetch:
        operands[2] = pltpu.with_memory_space_constraint(weight, pltpu.HBM)
    if bring is not None:
        operands.append(pltpu.with_memory_space_constraint(bring, pltpu.HBM))
        in_specs.append(HBM)
        out_shape.append(jax.ShapeDtypeStruct(bring.shape, bring.dtype))
        scratch.append(pltpu.SemaphoreType.DMA(()))
    return pl.pallas_call(
        body,
        in_specs=in_specs,
        out_specs=[VMEM] * len(out_shape),
        out_shape=out_shape,
        scratch_shapes=scratch,
        compiler_params=PARAMS,
        cost_estimate=QUICK,
        name="input_term",
    )(*operands)


def sum_call(table, mine, other):
    def body(table_ref, a, b, out):
        out[...] = (a[...].astype(F32) + b[...].astype(F32)).astype(BF16)

    return pl.pallas_call(
        body,
        in_specs=[SMEM, VMEM, VMEM],
        out_specs=VMEM,
        out_shape=jax.ShapeDtypeStruct(mine.shape, BF16),
        compiler_params=PARAMS,
        cost_estimate=QUICK,
        name="input_sum",
    )(table, mine, other)


def pair_call(table, a, b):
    def body(table_ref, a_ref, b_ref, out):
        out[0] = a_ref[...]
        out[1] = b_ref[...]

    return pl.pallas_call(
        body,
        in_specs=[SMEM, VMEM, VMEM],
        out_specs=VMEM,
        out_shape=jax.ShapeDtypeStruct((2, *a.shape), BF16),
        compiler_params=PARAMS,
        cost_estimate=QUICK,
        name="input_pair",
    )(table, a, b)


def put_call(table, out, width, unit, halves):
    n_tok = halves[0][1].shape[1]
    both = len(halves) == 2

    def body(table_ref, *refs):
        for (dh, _), ref in zip(halves, refs):
            for dq in range(2):
                quarter = table_ref[t_at(dh, dq)]
                start = pl.multiple_of((quarter if both else quarter % 2) * QUARTER, QUARTER)
                refs[-1][:, pl.ds(start, QUARTER)] = ref[dq]

    def place(j, t):
        return (0, unit) if both else (0, unit * 2 + t[t_at(halves[0][0], 0)] // 2)

    return pl.pallas_call(
        body,
        grid_spec=pltpu.PrefetchScalarGridSpec(
            num_scalar_prefetch=1,
            grid=(1,),
            in_specs=[VMEM] * len(halves) + [pl.BlockSpec(memory_space=pl.ANY)] * (out is not None),
            out_specs=pl.BlockSpec((n_tok, UNIT if both else UNIT // 2), place),
        ),
        out_shape=jax.ShapeDtypeStruct((n_tok, width), BF16),
        input_output_aliases={} if out is None else {1 + len(halves): 0},
        compiler_params=PARAMS,
        cost_estimate=QUICK,
        name="place_unit" if both else "place_half",
    )(table, *[half for _, half in halves], *([] if out is None else [out]))


def per_device(tokens, gate_pre, gated_cot, gate_weight):
    dp, tensor = lax.axis_index("dp"), lax.axis_index("tensor")
    x, zlo, core, y = dp // 4, dp // 2 % 2, dp % 2, tensor % 4
    n_tok, width = tokens.shape
    hidden = gate_pre.shape[1]

    def bits(i):
        return (i + 1) // 2 % 2, i // 2

    xor = jnp.bitwise_xor

    def in_order(first, second):
        return jnp.where(core == 0, first, second), jnp.where(core == 0, second, first)

    (ux, vx), (h, q) = bits(x), in_order(*bits(y))
    entries = []
    for d1 in (1, 0):
        for d2 in range(2):
            for half in range(2):
                du, dv = in_order(d1, d2)
                owner = xor(xor(ux, du), 3 * xor(vx, dv))
                entries.append(owner * 4 + xor(zlo, half) * 2 + core)
    entries += [xor(h, dh) * 2 + xor(q, dq) for dh in range(2) for dq in range(2)]
    table = jnp.stack(entries).astype(jnp.int32)

    last = [table]

    def ordered():
        return lax.optimization_barrier((table, last[0]))[0]

    their_tok = lax.ppermute(tokens, "dp", CORE_SWAP)
    if GATE_KERNEL:
        gate_cot = gate_call(gate_pre, gated_cot)
    else:
        gate_val = gate_pre.astype(F32)
        cot_val = gated_cot.astype(F32)
        sigmoid_val = 1.0 / (1.0 + jnp.exp(-gate_val))
        gate_cot = (cot_val * sigmoid_val * (1.0 + gate_val * (1.0 - sigmoid_val))).astype(BF16)
    their_cot = lax.ppermute(gate_cot, "dp", CORE_SWAP)

    def t_call(*args, **more):
        res = input_call(ordered(), gate_cot, more.pop("rows", gate_weight), *args, **more)
        last[0] = res[0]
        return res[0] if len(res) == 1 else res

    def g_call(*args):
        last[0] = weight_call(ordered(), shared.data, *args)[0]
        return last[0]

    def y_swap(value, step):
        return lax.ppermute(value, ("dp", "tensor"), Y_SWAP[step])

    def x_swap(value, step):
        return lax.ppermute(value, "dp", X_SWAP[step])

    def z_swap(value):
        return lax.ppermute(value, "dp", ZLO_SWAP)

    class Shared:
        pass

    shared = Shared()
    shared.tok = tokens

    def pack_first():
        ahead, both = pack_call(ordered(), 0, shared.tok, their_tok, [gate_cot, their_cot])
        last[0] = ahead
        shared.data = [ahead, both]

    def pack_second():
        last[0] = pack_call(ordered(), 4, shared.tok, their_tok, [])[0]
        shared.data.insert(1, last[0])

    class Unit:
        def __init__(self, unit):
            self.unit = unit

    def t_first(g, fetch=False):
        jobs = [(t_at(1, 0), []), (t_at(1, 1), [])]
        if fetch and SLICE:
            start = g.unit * UNIT + (1 - h) * 2 * QUARTER
            rows = lax.dynamic_slice(gate_weight, (start, 0), (2 * QUARTER, hidden))
            g.one = y_swap(t_call(g.unit, jobs, 2, False, rows=rows, local=True), 0)
        else:
            g.one = y_swap(t_call(g.unit, jobs, 2, fetch), 0)

    def t_second(g):
        g.two = y_swap(t_call(g.unit, [(t_at(0, 1), [(g.one, 1)])], 1, False), 1)

    def t_third(g):
        g.mine = t_call(g.unit, [(t_at(0, 0), [(g.one, 0), (g.two, None)])], 1, False)
        g.other = lax.ppermute(g.mine, "tensor", ZHI_SWAP)

    def t_fourth(g):
        last[0] = g.done = sum_call(ordered(), g.mine, g.other)
        g.near = y_swap(g.done, 1)

    def t_fifth(g):
        last[0] = g.half = pair_call(ordered(), g.done, g.near)
        g.far = y_swap(g.half, 0)

    def t_place(g, which, out):
        halves = [(dh, g.far if dh else g.half) for dh in which]
        last[0] = put_call(ordered(), out, width, g.unit, halves)
        return last[0]

    class Part:
        def __init__(self, cols):
            self.cols = cols

    def g_first(g):
        jobs = [(g_at(half, 1, d2), []) for d2 in range(2) for half in range(2)]
        g.one = x_swap(g_call(jobs, g.cols, [4]), 0)

    def g_second(g):
        jobs = [(g_at(half, 0, 1), [(g.one, 2 + half)]) for half in range(2)]
        g.two = x_swap(g_call(jobs, g.cols, [2]), 1)

    def g_third(g):
        g.other = z_swap(g_call([(g_at(1, 0, 0), [(g.one, 1), (g.two, 1)])], g.cols, [1]))
        g.adds = [(g.one, 0), (g.two, 0), (g.other, None)]

    def z_first(g):
        g.over = z_swap(g_call([(g_at(1, d1, d2), []) for d1 in range(2) for d2 in range(2)], g.cols, [4]))

    def z_second(g):
        g.one = x_swap(g_call([(g_at(0, 1, d2), [(g.over, 2 + d2)]) for d2 in range(2)], g.cols, [2]), 0)

    def z_third(g):
        g.two = x_swap(g_call([(g_at(0, 0, 1), [(g.over, 1), (g.one, 1)])], g.cols, [1]), 1)
        g.adds = [(g.over, 0), (g.one, 0), (g.two, None)]

    factor = 1.0 / math.sqrt(n_tok * lax.axis_size("dp"))

    def g_final(parts, grad):
        last[0] = final_call(ordered(), *shared.data[1:], [(g.cols, g.adds) for g in parts], factor, grad)
        return last[0]

    a, b = Unit(0), Unit(1)
    k, l, m = (Part(cols) for cols in COLS)
    steps = {
        "a1": lambda: t_first(a, FETCH),
        "b1": lambda: t_first(b),
        "P1": pack_first,
        "P2": pack_second,
    }
    for name, g in (("a", a), ("b", b)):
        for i, f in ((2, t_second), (3, t_third), (4, t_fourth), (5, t_fifth)):
            steps[f"{name}{i}"] = lambda f=f, g=g: f(g)
    for name, g in (("k", k), ("l", l), ("m", m)):
        forms = (z_first, z_second, z_third) if name == "m" and Z_FIRST else (g_first, g_second, g_third)
        for i, f in zip((1, 2, 3), forms):
            steps[f"{name}{i}"] = lambda f=f, g=g: f(g)
    for name, g in (("a", a), ("b", b), ("k", k), ("l", l), ("m", m)):
        for i, what in enumerate(("one", "two", "other", "near", "far")):
            steps[f"w{name}{i + 1}"] = lambda g=g, what=what: last.insert(0, (last[0], getattr(g, what)))
    done = {}
    for name, g, which in (("a7", a, (0, 1)), ("b6", b, (0,)), ("b7", b, (1,))):
        steps[name] = lambda g=g, which=which: done.update(out=t_place(g, which, done.get("out")))
    steps["kl4"] = lambda: done.update(grad=g_final([k, l], done.get("grad")))
    steps["m4"] = lambda: done.update(grad=g_final([m], done.get("grad")))
    for step in ORDER.split():
        steps[step]()
    return (done["out"], done["grad"])


def solution(mesh):
    placed = (P("dp", None), P("dp", "tensor"), P("dp", "tensor"), P(None, "tensor"))
    return jax.shard_map(
        per_device,
        mesh=mesh,
        in_specs=placed,
        out_specs=(P("dp", None), P("dp", "tensor")),
        check_vma=False,
    )
```

```python
import math

import jax
import jax.numpy as jnp
from jax import lax
from jax.experimental import pallas as pl
from jax.experimental.pallas import tpu as pltpu
from jax.sharding import PartitionSpec as P

CORE_SWAP = [(d, d ^ 1) for d in range(16)]
ZLO_SWAP = [(d, d ^ 2) for d in range(16)]
ZHI_SWAP = [(t, t ^ 4) for t in range(8)]


def over(i, which):
    return 3 - i if which else i ^ 1


X_SWAP = [[(d, over(d // 4, d % 2 ^ step) * 4 + d % 4) for d in range(16)] for step in range(2)]
Y_SWAP = [
    [(d * 8 + t, d * 8 + t // 4 * 4 + over(t % 4, d % 2 ^ step)) for d in range(16) for t in range(8)]
    for step in range(2)
]
BF16, F32 = jnp.bfloat16, jnp.float32
PARAMS = pltpu.CompilerParams(vmem_limit_bytes=12 * 2**20)
BLOCK = 256
QUARTER = 512
UNIT = 4 * QUARTER
FETCH = True
GATE_KERNEL = False
Z_FIRST = False
SLICE = True
COLS = ((0, 768), (768, 1536), (1536, 1920))
ORDER = (
    "a1", "P1", "k1", "b1", "P2", "l1", "a2", "b2", "a3", "k2", "m1", "b3",
    "a4", "l2", "b4", "a5", "k3", "l3", "wa1", "wk1", "b5", "m2", "a7", "wl3",
    "m3", "b6", "b7", "kl4", "wa5", "wb2", "m4",
)
VMEM = pl.BlockSpec(memory_space=pltpu.VMEM)
SMEM = pl.BlockSpec(memory_space=pltpu.SMEM)
HBM = pl.BlockSpec(memory_space=pltpu.HBM)
QUICK = pl.CostEstimate(flops=0, transcendentals=0, bytes_accessed=0)
G_AT, T_AT = 0, 8


def g_at(half, d1, d2):
    return G_AT + (1 - d1) * 4 + d2 * 2 + half


def t_at(dh, dq):
    return T_AT + dh * 2 + dq


def gate_call(gate_pre, gated_cot):
    n_tok, hidden = gate_pre.shape
    rows = 64

    def body(pre_ref, cot_ref, out_ref):
        gate_val = pre_ref[...].astype(F32)
        cot_val = cot_ref[...].astype(F32)
        sigmoid_val = 1.0 / (1.0 + jnp.exp(-gate_val))
        out_ref[...] = (cot_val * sigmoid_val * (1.0 + gate_val * (1.0 - sigmoid_val))).astype(BF16)

    block = pl.BlockSpec((rows, hidden), lambda j: (j, 0))
    return pl.pallas_call(
        body,
        grid=(n_tok // rows,),
        in_specs=[block, block],
        out_specs=block,
        out_shape=jax.ShapeDtypeStruct((n_tok, hidden), BF16),
        compiler_params=PARAMS,
        cost_estimate=QUICK,
        name="gate_cot",
    )(gate_pre, gated_cot)


def pack_call(table, first, tok, their_tok, cots):
    n_tok = tok.shape[0]

    def body(table_ref, tok_ref, their_tok_ref, *refs):
        turned = refs[len(cots)]
        for n in range(4):
            here = pl.ds(pl.multiple_of(table_ref[G_AT + first + n] * BLOCK, BLOCK), BLOCK)
            turned[n, :, :n_tok] = tok_ref[:, here].T
            turned[n, :, n_tok:] = their_tok_ref[:, here].T
        for n in range(len(cots)):
            refs[-1][n * n_tok : (n + 1) * n_tok] = refs[n][...]

    shapes = [jax.ShapeDtypeStruct((4, BLOCK, 2 * n_tok), BF16)]
    if cots:
        shapes.append(jax.ShapeDtypeStruct((2 * n_tok, cots[0].shape[1]), BF16))
    return pl.pallas_call(
        body,
        in_specs=[SMEM] + [VMEM] * (2 + len(cots)),
        out_specs=[VMEM] * len(shapes),
        out_shape=shapes,
        compiler_params=PARAMS,
        cost_estimate=QUICK,
        name="pack",
    )(table, tok, pltpu.with_memory_space_constraint(their_tok, pltpu.VMEM), *cots)


def weight_call(table, data, jobs, cols, outs):
    flat = [a for _, adds in jobs for a in adds]
    lo, hi = cols

    def body(table_ref, *refs):
        n = len(data) - 1
        turned, both, refs = refs[:n], refs[n], refs[n + 1 :]
        added = iter(zip(refs, flat))
        out_refs = refs[len(flat) :]
        slots = [(o, i) for o, n in enumerate(outs) for i in range(n)]
        for (at, adds), (o, i) in zip(jobs, slots):
            value = jnp.dot(turned[at // 4][at % 4], both[:, lo:hi], preferred_element_type=F32)
            for _ in adds:
                ref, (_, index) = next(added)
                value += (ref[...] if index is None else ref[index]).astype(F32)
            if outs[o] == 1:
                out_refs[o][...] = value.astype(BF16)
            else:
                out_refs[o][i] = value.astype(BF16)

    return pl.pallas_call(
        body,
        in_specs=[SMEM] + [VMEM] * (len(data) + len(flat)),
        out_specs=[VMEM] * len(outs),
        out_shape=[
            jax.ShapeDtypeStruct((BLOCK, hi - lo) if n == 1 else (n, BLOCK, hi - lo), BF16) for n in outs
        ],
        compiler_params=PARAMS,
        cost_estimate=QUICK,
        name="weight_term",
    )(table, *data, *[a for a, _ in flat])


def final_call(table, turned, both, parts, factor, into):
    tile = parts[0][0][1] - parts[0][0][0]
    hidden = both.shape[1]
    flat, tiles = [], []
    for (lo, hi), adds in parts:
        which = range(len(flat), len(flat) + len(adds))
        tiles += [(start, start - lo, which) for start in range(lo, hi, tile)]
        flat += adds

    def body(table_ref, turned_ref, both_ref, *refs):
        for j, (start, inner, which) in enumerate(tiles):

            @pl.when(pl.program_id(0) == j)
            def _():
                here = slice(inner, inner + tile)
                value = jnp.dot(turned_ref[0], both_ref[:, start : start + tile], preferred_element_type=F32)
                for k in which:
                    index = flat[k][1]
                    value += (refs[k][:, here] if index is None else refs[k][index, :, here]).astype(F32)
                refs[-1][...] = value * factor

    first = tiles[0][0] // tile
    return pl.pallas_call(
        body,
        grid=(len(tiles),),
        in_specs=[SMEM] + [VMEM] * (2 + len(flat)) + [pl.BlockSpec(memory_space=pl.ANY)] * (into is not None),
        out_specs=pl.BlockSpec((BLOCK, tile), lambda j: (0, first + j)),
        out_shape=jax.ShapeDtypeStruct((BLOCK, hidden), F32),
        input_output_aliases={} if into is None else {3 + len(flat): 0},
        compiler_params=PARAMS,
        cost_estimate=QUICK,
        name="weight_grad",
    )(table, turned, both, *[a for a, _ in flat], *([] if into is None else [into]))


def input_call(table, cot, weight, unit, jobs, n_out, fetch, bring=None, local=False):
    flat = [a for _, adds in jobs for a in adds]
    n_tok, hidden = cot.shape
    half = QUARTER // 2

    def body(table_ref, cot_ref, w_ref, *refs):
        added = iter(zip(refs, flat))
        refs = refs[len(flat) :]
        if bring is not None:
            brought = pltpu.make_async_copy(refs[0], refs[2], refs[-1])
            out, refs = refs[1], refs[3:-1]
        else:
            out, refs = refs[0], refs[1:]

        def rows(at, part):
            start = (table_ref[at] % 2 if local else unit * (UNIT // QUARTER) + table_ref[at]) * QUARTER + part * half
            return pl.ds(pl.multiple_of(start, half), half)

        parts = [(k, part) for k in range(len(jobs)) for part in range(2)]
        copies = []
        if fetch:
            buf, sems = refs
            for n, (k, part) in enumerate(parts):
                copies.append(pltpu.make_async_copy(w_ref.at[rows(jobs[k][0], part)], buf.at[n], sems.at[n]))
            for copy in copies:
                copy.start()
        if bring is not None:
            brought.start()
        for n, (k, part) in enumerate(parts):
            if part == 0:
                extras = [next(added) for _ in jobs[k][1]]
            if fetch:
                copies[n].wait()
            w = buf[n] if fetch else w_ref[rows(jobs[k][0], part)]
            value = lax.dot_general(cot_ref[...], w, (((1,), (1,)), ((), ())), preferred_element_type=F32)
            here = slice(part * half, (part + 1) * half)
            for ref, (_, index) in extras:
                value += (ref[:, here] if index is None else ref[index, :, here]).astype(F32)
            if n_out == 1:
                out[:, here] = value.astype(BF16)
            else:
                out[k, :, here] = value.astype(BF16)
        if bring is not None:
            brought.wait()

    n = 2 * len(jobs)
    scratch = [pltpu.VMEM((n, half, hidden), BF16), pltpu.SemaphoreType.DMA((n,))] if fetch else []
    operands = [table, cot, weight, *[a for a, _ in flat]]
    in_specs = [SMEM, VMEM, HBM if fetch else VMEM] + [VMEM] * len(flat)
    out_shape = [jax.ShapeDtypeStruct((n_tok, QUARTER) if n_out == 1 else (n_out, n_tok, QUARTER), BF16)]
    if fetch:
        operands[2] = pltpu.with_memory_space_constraint(weight, pltpu.HBM)
    if bring is not None:
        operands.append(pltpu.with_memory_space_constraint(bring, pltpu.HBM))
        in_specs.append(HBM)
        out_shape.append(jax.ShapeDtypeStruct(bring.shape, bring.dtype))
        scratch.append(pltpu.SemaphoreType.DMA(()))
    return pl.pallas_call(
        body,
        in_specs=in_specs,
        out_specs=[VMEM] * len(out_shape),
        out_shape=out_shape,
        scratch_shapes=scratch,
        compiler_params=PARAMS,
        cost_estimate=QUICK,
        name="input_term",
    )(*operands)


def sum_call(table, mine, other):
    def body(table_ref, a, b, out):
        out[...] = (a[...].astype(F32) + b[...].astype(F32)).astype(BF16)

    return pl.pallas_call(
        body,
        in_specs=[SMEM, VMEM, VMEM],
        out_specs=VMEM,
        out_shape=jax.ShapeDtypeStruct(mine.shape, BF16),
        compiler_params=PARAMS,
        cost_estimate=QUICK,
        name="input_sum",
    )(table, mine, other)


def pair_call(table, a, b):
    def body(table_ref, a_ref, b_ref, out):
        out[0] = a_ref[...]
        out[1] = b_ref[...]

    return pl.pallas_call(
        body,
        in_specs=[SMEM, VMEM, VMEM],
        out_specs=VMEM,
        out_shape=jax.ShapeDtypeStruct((2, *a.shape), BF16),
        compiler_params=PARAMS,
        cost_estimate=QUICK,
        name="input_pair",
    )(table, a, b)


def put_call(table, out, width, unit, halves):
    n_tok = halves[0][1].shape[1]
    both = len(halves) == 2

    def body(table_ref, *refs):
        for (dh, _), ref in zip(halves, refs):
            for dq in range(2):
                quarter = table_ref[t_at(dh, dq)]
                start = pl.multiple_of((quarter if both else quarter % 2) * QUARTER, QUARTER)
                refs[-1][:, pl.ds(start, QUARTER)] = ref[dq]

    def place(j, t):
        return (0, unit) if both else (0, unit * 2 + t[t_at(halves[0][0], 0)] // 2)

    return pl.pallas_call(
        body,
        grid_spec=pltpu.PrefetchScalarGridSpec(
            num_scalar_prefetch=1,
            grid=(1,),
            in_specs=[VMEM] * len(halves) + [pl.BlockSpec(memory_space=pl.ANY)] * (out is not None),
            out_specs=pl.BlockSpec((n_tok, UNIT if both else UNIT // 2), place),
        ),
        out_shape=jax.ShapeDtypeStruct((n_tok, width), BF16),
        input_output_aliases={} if out is None else {1 + len(halves): 0},
        compiler_params=PARAMS,
        cost_estimate=QUICK,
        name="place_unit" if both else "place_half",
    )(table, *[half for _, half in halves], *([] if out is None else [out]))


def per_device(tokens, gate_pre, gated_cot, gate_weight):
    dp, tensor = lax.axis_index("dp"), lax.axis_index("tensor")
    x, zlo, core, y = dp // 4, dp // 2 % 2, dp % 2, tensor % 4
    n_tok, width = tokens.shape
    hidden = gate_pre.shape[1]

    def bits(i):
        return (i + 1) // 2 % 2, i // 2

    xor = jnp.bitwise_xor

    def in_order(first, second):
        return jnp.where(core == 0, first, second), jnp.where(core == 0, second, first)

    (ux, vx), (h, q) = bits(x), in_order(*bits(y))
    entries = []
    for d1 in (1, 0):
        for d2 in range(2):
            for half in range(2):
                du, dv = in_order(d1, d2)
                owner = xor(xor(ux, du), 3 * xor(vx, dv))
                entries.append(owner * 4 + xor(zlo, half) * 2 + core)
    entries += [xor(h, dh) * 2 + xor(q, dq) for dh in range(2) for dq in range(2)]
    table = jnp.stack(entries).astype(jnp.int32)

    last = [table]

    def ordered():
        return lax.optimization_barrier((table, last[0]))[0]

    their_tok = lax.ppermute(tokens, "dp", CORE_SWAP)
    if GATE_KERNEL:
        gate_cot = gate_call(gate_pre, gated_cot)
    else:
        gate_val = gate_pre.astype(F32)
        cot_val = gated_cot.astype(F32)
        sigmoid_val = 1.0 / (1.0 + jnp.exp(-gate_val))
        gate_cot = (cot_val * sigmoid_val * (1.0 + gate_val * (1.0 - sigmoid_val))).astype(BF16)
    their_cot = lax.ppermute(gate_cot, "dp", CORE_SWAP)

    def t_call(*args, **more):
        res = input_call(ordered(), gate_cot, more.pop("rows", gate_weight), *args, **more)
        last[0] = res[0]
        return res[0] if len(res) == 1 else res

    def g_call(*args):
        last[0] = weight_call(ordered(), shared.data, *args)[0]
        return last[0]

    def y_swap(value, step):
        return lax.ppermute(value, ("dp", "tensor"), Y_SWAP[step])

    def x_swap(value, step):
        return lax.ppermute(value, "dp", X_SWAP[step])

    def z_swap(value):
        return lax.ppermute(value, "dp", ZLO_SWAP)

    class Shared:
        pass

    shared = Shared()
    shared.tok = tokens

    def pack_first():
        ahead, both = pack_call(ordered(), 0, shared.tok, their_tok, [gate_cot, their_cot])
        last[0] = ahead
        shared.data = [ahead, both]

    def pack_second():
        last[0] = pack_call(ordered(), 4, shared.tok, their_tok, [])[0]
        shared.data.insert(1, last[0])

    class Unit:
        def __init__(self, unit):
            self.unit = unit

    def t_first(g, fetch=False):
        jobs = [(t_at(1, 0), []), (t_at(1, 1), [])]
        if fetch and SLICE:
            start = g.unit * UNIT + (1 - h) * 2 * QUARTER
            rows = lax.dynamic_slice(gate_weight, (start, 0), (2 * QUARTER, hidden))
            g.one = y_swap(t_call(g.unit, jobs, 2, False, rows=rows, local=True), 0)
        else:
            g.one = y_swap(t_call(g.unit, jobs, 2, fetch), 0)

    def t_second(g):
        g.two = y_swap(t_call(g.unit, [(t_at(0, 1), [(g.one, 1)])], 1, False), 1)

    def t_third(g):
        g.mine = t_call(g.unit, [(t_at(0, 0), [(g.one, 0), (g.two, None)])], 1, False)
        g.other = lax.ppermute(g.mine, "tensor", ZHI_SWAP)

    def t_fourth(g):
        last[0] = g.done = sum_call(ordered(), g.mine, g.other)
        g.near = y_swap(g.done, 1)

    def t_fifth(g):
        last[0] = g.half = pair_call(ordered(), g.done, g.near)
        g.far = y_swap(g.half, 0)

    def t_place(g, which, out):
        halves = [(dh, g.far if dh else g.half) for dh in which]
        last[0] = put_call(ordered(), out, width, g.unit, halves)
        return last[0]

    class Part:
        def __init__(self, cols):
            self.cols = cols

    def g_first(g):
        jobs = [(g_at(half, 1, d2), []) for d2 in range(2) for half in range(2)]
        g.one = x_swap(g_call(jobs, g.cols, [4]), 0)

    def g_second(g):
        jobs = [(g_at(half, 0, 1), [(g.one, 2 + half)]) for half in range(2)]
        g.two = x_swap(g_call(jobs, g.cols, [2]), 1)

    def g_third(g):
        g.other = z_swap(g_call([(g_at(1, 0, 0), [(g.one, 1), (g.two, 1)])], g.cols, [1]))
        g.adds = [(g.one, 0), (g.two, 0), (g.other, None)]

    def z_first(g):
        g.over = z_swap(g_call([(g_at(1, d1, d2), []) for d1 in range(2) for d2 in range(2)], g.cols, [4]))

    def z_second(g):
        g.one = x_swap(g_call([(g_at(0, 1, d2), [(g.over, 2 + d2)]) for d2 in range(2)], g.cols, [2]), 0)

    def z_third(g):
        g.two = x_swap(g_call([(g_at(0, 0, 1), [(g.over, 1), (g.one, 1)])], g.cols, [1]), 1)
        g.adds = [(g.over, 0), (g.one, 0), (g.two, None)]

    factor = 1.0 / math.sqrt(n_tok * lax.axis_size("dp"))

    def g_final(parts, grad):
        last[0] = final_call(ordered(), *shared.data[1:], [(g.cols, g.adds) for g in parts], factor, grad)
        return last[0]

    a, b = Unit(0), Unit(1)
    k, l, m = (Part(cols) for cols in COLS)
    steps = {
        "a1": lambda: t_first(a, FETCH),
        "b1": lambda: t_first(b),
        "P1": pack_first,
        "P2": pack_second,
    }
    for name, g in (("a", a), ("b", b)):
        for i, f in ((2, t_second), (3, t_third), (4, t_fourth), (5, t_fifth)):
            steps[f"{name}{i}"] = lambda f=f, g=g: f(g)
    for name, g in (("k", k), ("l", l), ("m", m)):
        forms = (z_first, z_second, z_third) if name == "m" and Z_FIRST else (g_first, g_second, g_third)
        for i, f in zip((1, 2, 3), forms):
            steps[f"{name}{i}"] = lambda f=f, g=g: f(g)
    for name, g in (("a", a), ("b", b), ("k", k), ("l", l), ("m", m)):
        for i, what in enumerate(("one", "two", "other", "near", "far")):
            steps[f"w{name}{i + 1}"] = lambda g=g, what=what: last.insert(0, (last[0], getattr(g, what)))
    done = {}
    for name, g, which in (("a7", a, (0, 1)), ("b6", b, (0,)), ("b7", b, (1,))):
        steps[name] = lambda g=g, which=which: done.update(out=t_place(g, which, done.get("out")))
    steps["kl4"] = lambda: done.update(grad=g_final([k, l], done.get("grad")))
    steps["m4"] = lambda: done.update(grad=g_final([m], done.get("grad")))
    for step in ORDER:
        steps[step]()
    return (done["out"], done["grad"])


def solution(mesh):
    placed = (P("dp", None), P("dp", "tensor"), P("dp", "tensor"), P(None, "tensor"))
    return jax.shard_map(
        per_device,
        mesh=mesh,
        in_specs=placed,
        out_specs=(P("dp", None), P("dp", "tensor")),
        check_vma=False,
    )
```

```python
import math

import jax
import jax.numpy as jnp
from jax import lax
from jax.experimental import pallas as pl
from jax.experimental.pallas import tpu as pltpu
from jax.sharding import PartitionSpec as P

CORE_SWAP = [(d, d ^ 1) for d in range(16)]
ZLO_SWAP = [(d, d ^ 2) for d in range(16)]
ZHI_SWAP = [(t, t ^ 4) for t in range(8)]


def over(i, which):
    return 3 - i if which else i ^ 1


X_SWAP = [[(d, over(d // 4, d % 2 ^ step) * 4 + d % 4) for d in range(16)] for step in range(2)]
Y_SWAP = [
    [(d * 8 + t, d * 8 + t // 4 * 4 + over(t % 4, d % 2 ^ step)) for d in range(16) for t in range(8)]
    for step in range(2)
]
BF16, F32 = jnp.bfloat16, jnp.float32
PARAMS = pltpu.CompilerParams(vmem_limit_bytes=12 * 2**20)
BLOCK = 256
QUARTER = 512
UNIT = 4 * QUARTER
FETCH = True
GATE_KERNEL = False
Z_FIRST = False
SLICE = True
COLS = ((0, 768), (768, 1536), (1536, 1920))
ORDER = (
    "a1", "P1", "k1", "b1", "P2", "l1", "a2", "b2", "a3", "k2", "b3", "a4",
    "l2", "m1", "b4", "a5", "k3", "l3", "wa1", "wk1", "b5", "m2", "a7", "wl3",
    "m3", "b6", "b7", "kl4", "wa5", "wb2", "m4",
)
VMEM = pl.BlockSpec(memory_space=pltpu.VMEM)
SMEM = pl.BlockSpec(memory_space=pltpu.SMEM)
HBM = pl.BlockSpec(memory_space=pltpu.HBM)
QUICK = pl.CostEstimate(flops=0, transcendentals=0, bytes_accessed=0)
G_AT, T_AT = 0, 8


def g_at(half, d1, d2):
    return G_AT + (1 - d1) * 4 + d2 * 2 + half


def t_at(dh, dq):
    return T_AT + dh * 2 + dq


def gate_call(gate_pre, gated_cot):
    n_tok, hidden = gate_pre.shape
    rows = 64

    def body(pre_ref, cot_ref, out_ref):
        gate_val = pre_ref[...].astype(F32)
        cot_val = cot_ref[...].astype(F32)
        sigmoid_val = 1.0 / (1.0 + jnp.exp(-gate_val))
        out_ref[...] = (cot_val * sigmoid_val * (1.0 + gate_val * (1.0 - sigmoid_val))).astype(BF16)

    block = pl.BlockSpec((rows, hidden), lambda j: (j, 0))
    return pl.pallas_call(
        body,
        grid=(n_tok // rows,),
        in_specs=[block, block],
        out_specs=block,
        out_shape=jax.ShapeDtypeStruct((n_tok, hidden), BF16),
        compiler_params=PARAMS,
        cost_estimate=QUICK,
        name="gate_cot",
    )(gate_pre, gated_cot)


def pack_call(table, first, tok, their_tok, cots):
    n_tok = tok.shape[0]

    def body(table_ref, tok_ref, their_tok_ref, *refs):
        turned = refs[len(cots)]
        for n in range(4):
            here = pl.ds(pl.multiple_of(table_ref[G_AT + first + n] * BLOCK, BLOCK), BLOCK)
            turned[n, :, :n_tok] = tok_ref[:, here].T
            turned[n, :, n_tok:] = their_tok_ref[:, here].T
        for n in range(len(cots)):
            refs[-1][n * n_tok : (n + 1) * n_tok] = refs[n][...]

    shapes = [jax.ShapeDtypeStruct((4, BLOCK, 2 * n_tok), BF16)]
    if cots:
        shapes.append(jax.ShapeDtypeStruct((2 * n_tok, cots[0].shape[1]), BF16))
    return pl.pallas_call(
        body,
        in_specs=[SMEM] + [VMEM] * (2 + len(cots)),
        out_specs=[VMEM] * len(shapes),
        out_shape=shapes,
        compiler_params=PARAMS,
        cost_estimate=QUICK,
        name="pack",
    )(table, tok, pltpu.with_memory_space_constraint(their_tok, pltpu.VMEM), *cots)


def weight_call(table, data, jobs, cols, outs):
    flat = [a for _, adds in jobs for a in adds]
    lo, hi = cols

    def body(table_ref, *refs):
        n = len(data) - 1
        turned, both, refs = refs[:n], refs[n], refs[n + 1 :]
        added = iter(zip(refs, flat))
        out_refs = refs[len(flat) :]
        slots = [(o, i) for o, n in enumerate(outs) for i in range(n)]
        for (at, adds), (o, i) in zip(jobs, slots):
            value = jnp.dot(turned[at // 4][at % 4], both[:, lo:hi], preferred_element_type=F32)
            for _ in adds:
                ref, (_, index) = next(added)
                value += (ref[...] if index is None else ref[index]).astype(F32)
            if outs[o] == 1:
                out_refs[o][...] = value.astype(BF16)
            else:
                out_refs[o][i] = value.astype(BF16)

    return pl.pallas_call(
        body,
        in_specs=[SMEM] + [VMEM] * (len(data) + len(flat)),
        out_specs=[VMEM] * len(outs),
        out_shape=[
            jax.ShapeDtypeStruct((BLOCK, hi - lo) if n == 1 else (n, BLOCK, hi - lo), BF16) for n in outs
        ],
        compiler_params=PARAMS,
        cost_estimate=QUICK,
        name="weight_term",
    )(table, *data, *[a for a, _ in flat])


def final_call(table, turned, both, parts, factor, into):
    tile = parts[0][0][1] - parts[0][0][0]
    hidden = both.shape[1]
    flat, tiles = [], []
    for (lo, hi), adds in parts:
        which = range(len(flat), len(flat) + len(adds))
        tiles += [(start, start - lo, which) for start in range(lo, hi, tile)]
        flat += adds

    def body(table_ref, turned_ref, both_ref, *refs):
        for j, (start, inner, which) in enumerate(tiles):

            @pl.when(pl.program_id(0) == j)
            def _():
                here = slice(inner, inner + tile)
                value = jnp.dot(turned_ref[0], both_ref[:, start : start + tile], preferred_element_type=F32)
                for k in which:
                    index = flat[k][1]
                    value += (refs[k][:, here] if index is None else refs[k][index, :, here]).astype(F32)
                refs[-1][...] = value * factor

    first = tiles[0][0] // tile
    return pl.pallas_call(
        body,
        grid=(len(tiles),),
        in_specs=[SMEM] + [VMEM] * (2 + len(flat)) + [pl.BlockSpec(memory_space=pl.ANY)] * (into is not None),
        out_specs=pl.BlockSpec((BLOCK, tile), lambda j: (0, first + j)),
        out_shape=jax.ShapeDtypeStruct((BLOCK, hidden), F32),
        input_output_aliases={} if into is None else {3 + len(flat): 0},
        compiler_params=PARAMS,
        cost_estimate=QUICK,
        name="weight_grad",
    )(table, turned, both, *[a for a, _ in flat], *([] if into is None else [into]))


def input_call(table, cot, weight, unit, jobs, n_out, fetch, bring=None, local=False):
    flat = [a for _, adds in jobs for a in adds]
    n_tok, hidden = cot.shape
    half = QUARTER // 2

    def body(table_ref, cot_ref, w_ref, *refs):
        added = iter(zip(refs, flat))
        refs = refs[len(flat) :]
        if bring is not None:
            brought = pltpu.make_async_copy(refs[0], refs[2], refs[-1])
            out, refs = refs[1], refs[3:-1]
        else:
            out, refs = refs[0], refs[1:]

        def rows(at, part):
            start = (table_ref[at] % 2 if local else unit * (UNIT // QUARTER) + table_ref[at]) * QUARTER + part * half
            return pl.ds(pl.multiple_of(start, half), half)

        parts = [(k, part) for k in range(len(jobs)) for part in range(2)]
        copies = []
        if fetch:
            buf, sems = refs
            for n, (k, part) in enumerate(parts):
                copies.append(pltpu.make_async_copy(w_ref.at[rows(jobs[k][0], part)], buf.at[n], sems.at[n]))
            for copy in copies:
                copy.start()
        if bring is not None:
            brought.start()
        for n, (k, part) in enumerate(parts):
            if part == 0:
                extras = [next(added) for _ in jobs[k][1]]
            if fetch:
                copies[n].wait()
            w = buf[n] if fetch else w_ref[rows(jobs[k][0], part)]
            value = lax.dot_general(cot_ref[...], w, (((1,), (1,)), ((), ())), preferred_element_type=F32)
            here = slice(part * half, (part + 1) * half)
            for ref, (_, index) in extras:
                value += (ref[:, here] if index is None else ref[index, :, here]).astype(F32)
            if n_out == 1:
                out[:, here] = value.astype(BF16)
            else:
                out[k, :, here] = value.astype(BF16)
        if bring is not None:
            brought.wait()

    n = 2 * len(jobs)
    scratch = [pltpu.VMEM((n, half, hidden), BF16), pltpu.SemaphoreType.DMA((n,))] if fetch else []
    operands = [table, cot, weight, *[a for a, _ in flat]]
    in_specs = [SMEM, VMEM, HBM if fetch else VMEM] + [VMEM] * len(flat)
    out_shape = [jax.ShapeDtypeStruct((n_tok, QUARTER) if n_out == 1 else (n_out, n_tok, QUARTER), BF16)]
    if fetch:
        operands[2] = pltpu.with_memory_space_constraint(weight, pltpu.HBM)
    if bring is not None:
        operands.append(pltpu.with_memory_space_constraint(bring, pltpu.HBM))
        in_specs.append(HBM)
        out_shape.append(jax.ShapeDtypeStruct(bring.shape, bring.dtype))
        scratch.append(pltpu.SemaphoreType.DMA(()))
    return pl.pallas_call(
        body,
        in_specs=in_specs,
        out_specs=[VMEM] * len(out_shape),
        out_shape=out_shape,
        scratch_shapes=scratch,
        compiler_params=PARAMS,
        cost_estimate=QUICK,
        name="input_term",
    )(*operands)


def sum_call(table, mine, other):
    def body(table_ref, a, b, out):
        out[...] = (a[...].astype(F32) + b[...].astype(F32)).astype(BF16)

    return pl.pallas_call(
        body,
        in_specs=[SMEM, VMEM, VMEM],
        out_specs=VMEM,
        out_shape=jax.ShapeDtypeStruct(mine.shape, BF16),
        compiler_params=PARAMS,
        cost_estimate=QUICK,
        name="input_sum",
    )(table, mine, other)


def pair_call(table, a, b):
    def body(table_ref, a_ref, b_ref, out):
        out[0] = a_ref[...]
        out[1] = b_ref[...]

    return pl.pallas_call(
        body,
        in_specs=[SMEM, VMEM, VMEM],
        out_specs=VMEM,
        out_shape=jax.ShapeDtypeStruct((2, *a.shape), BF16),
        compiler_params=PARAMS,
        cost_estimate=QUICK,
        name="input_pair",
    )(table, a, b)


def put_call(table, out, width, unit, halves):
    n_tok = halves[0][1].shape[1]
    both = len(halves) == 2

    def body(table_ref, *refs):
        for (dh, _), ref in zip(halves, refs):
            for dq in range(2):
                quarter = table_ref[t_at(dh, dq)]
                start = pl.multiple_of((quarter if both else quarter % 2) * QUARTER, QUARTER)
                refs[-1][:, pl.ds(start, QUARTER)] = ref[dq]

    def place(j, t):
        return (0, unit) if both else (0, unit * 2 + t[t_at(halves[0][0], 0)] // 2)

    return pl.pallas_call(
        body,
        grid_spec=pltpu.PrefetchScalarGridSpec(
            num_scalar_prefetch=1,
            grid=(1,),
            in_specs=[VMEM] * len(halves) + [pl.BlockSpec(memory_space=pl.ANY)] * (out is not None),
            out_specs=pl.BlockSpec((n_tok, UNIT if both else UNIT // 2), place),
        ),
        out_shape=jax.ShapeDtypeStruct((n_tok, width), BF16),
        input_output_aliases={} if out is None else {1 + len(halves): 0},
        compiler_params=PARAMS,
        cost_estimate=QUICK,
        name="place_unit" if both else "place_half",
    )(table, *[half for _, half in halves], *([] if out is None else [out]))


def per_device(tokens, gate_pre, gated_cot, gate_weight):
    dp, tensor = lax.axis_index("dp"), lax.axis_index("tensor")
    x, zlo, core, y = dp // 4, dp // 2 % 2, dp % 2, tensor % 4
    n_tok, width = tokens.shape
    hidden = gate_pre.shape[1]

    def bits(i):
        return (i + 1) // 2 % 2, i // 2

    xor = jnp.bitwise_xor

    def in_order(first, second):
        return jnp.where(core == 0, first, second), jnp.where(core == 0, second, first)

    (ux, vx), (h, q) = bits(x), in_order(*bits(y))
    entries = []
    for d1 in (1, 0):
        for d2 in range(2):
            for half in range(2):
                du, dv = in_order(d1, d2)
                owner = xor(xor(ux, du), 3 * xor(vx, dv))
                entries.append(owner * 4 + xor(zlo, half) * 2 + core)
    entries += [xor(h, dh) * 2 + xor(q, dq) for dh in range(2) for dq in range(2)]
    table = jnp.stack(entries).astype(jnp.int32)

    last = [table]

    def ordered():
        return lax.optimization_barrier((table, last[0]))[0]

    their_tok = lax.ppermute(tokens, "dp", CORE_SWAP)
    if GATE_KERNEL:
        gate_cot = gate_call(gate_pre, gated_cot)
    else:
        gate_val = gate_pre.astype(F32)
        cot_val = gated_cot.astype(F32)
        sigmoid_val = 1.0 / (1.0 + jnp.exp(-gate_val))
        gate_cot = (cot_val * sigmoid_val * (1.0 + gate_val * (1.0 - sigmoid_val))).astype(BF16)
    their_cot = lax.ppermute(gate_cot, "dp", CORE_SWAP)

    def t_call(*args, **more):
        res = input_call(ordered(), gate_cot, more.pop("rows", gate_weight), *args, **more)
        last[0] = res[0]
        return res[0] if len(res) == 1 else res

    def g_call(*args):
        last[0] = weight_call(ordered(), shared.data, *args)[0]
        return last[0]

    def y_swap(value, step):
        return lax.ppermute(value, ("dp", "tensor"), Y_SWAP[step])

    def x_swap(value, step):
        return lax.ppermute(value, "dp", X_SWAP[step])

    def z_swap(value):
        return lax.ppermute(value, "dp", ZLO_SWAP)

    class Shared:
        pass

    shared = Shared()
    shared.tok = tokens

    def pack_first():
        ahead, both = pack_call(ordered(), 0, shared.tok, their_tok, [gate_cot, their_cot])
        last[0] = ahead
        shared.data = [ahead, both]

    def pack_second():
        last[0] = pack_call(ordered(), 4, shared.tok, their_tok, [])[0]
        shared.data.insert(1, last[0])

    class Unit:
        def __init__(self, unit):
            self.unit = unit

    def t_first(g, fetch=False):
        jobs = [(t_at(1, 0), []), (t_at(1, 1), [])]
        if fetch and SLICE:
            start = g.unit * UNIT + (1 - h) * 2 * QUARTER
            rows = lax.dynamic_slice(gate_weight, (start, 0), (2 * QUARTER, hidden))
            g.one = y_swap(t_call(g.unit, jobs, 2, False, rows=rows, local=True), 0)
        else:
            g.one = y_swap(t_call(g.unit, jobs, 2, fetch), 0)

    def t_second(g):
        g.two = y_swap(t_call(g.unit, [(t_at(0, 1), [(g.one, 1)])], 1, False), 1)

    def t_third(g):
        g.mine = t_call(g.unit, [(t_at(0, 0), [(g.one, 0), (g.two, None)])], 1, False)
        g.other = lax.ppermute(g.mine, "tensor", ZHI_SWAP)

    def t_fourth(g):
        last[0] = g.done = sum_call(ordered(), g.mine, g.other)
        g.near = y_swap(g.done, 1)

    def t_fifth(g):
        last[0] = g.half = pair_call(ordered(), g.done, g.near)
        g.far = y_swap(g.half, 0)

    def t_place(g, which, out):
        halves = [(dh, g.far if dh else g.half) for dh in which]
        last[0] = put_call(ordered(), out, width, g.unit, halves)
        return last[0]

    class Part:
        def __init__(self, cols):
            self.cols = cols

    def g_first(g):
        jobs = [(g_at(half, 1, d2), []) for d2 in range(2) for half in range(2)]
        g.one = x_swap(g_call(jobs, g.cols, [4]), 0)

    def g_second(g):
        jobs = [(g_at(half, 0, 1), [(g.one, 2 + half)]) for half in range(2)]
        g.two = x_swap(g_call(jobs, g.cols, [2]), 1)

    def g_third(g):
        g.other = z_swap(g_call([(g_at(1, 0, 0), [(g.one, 1), (g.two, 1)])], g.cols, [1]))
        g.adds = [(g.one, 0), (g.two, 0), (g.other, None)]

    def z_first(g):
        g.over = z_swap(g_call([(g_at(1, d1, d2), []) for d1 in range(2) for d2 in range(2)], g.cols, [4]))

    def z_second(g):
        g.one = x_swap(g_call([(g_at(0, 1, d2), [(g.over, 2 + d2)]) for d2 in range(2)], g.cols, [2]), 0)

    def z_third(g):
        g.two = x_swap(g_call([(g_at(0, 0, 1), [(g.over, 1), (g.one, 1)])], g.cols, [1]), 1)
        g.adds = [(g.over, 0), (g.one, 0), (g.two, None)]

    factor = 1.0 / math.sqrt(n_tok * lax.axis_size("dp"))

    def g_final(parts, grad):
        last[0] = final_call(ordered(), *shared.data[1:], [(g.cols, g.adds) for g in parts], factor, grad)
        return last[0]

    a, b = Unit(0), Unit(1)
    k, l, m = (Part(cols) for cols in COLS)
    steps = {
        "a1": lambda: t_first(a, FETCH),
        "b1": lambda: t_first(b),
        "P1": pack_first,
        "P2": pack_second,
    }
    for name, g in (("a", a), ("b", b)):
        for i, f in ((2, t_second), (3, t_third), (4, t_fourth), (5, t_fifth)):
            steps[f"{name}{i}"] = lambda f=f, g=g: f(g)
    for name, g in (("k", k), ("l", l), ("m", m)):
        forms = (z_first, z_second, z_third) if name == "m" and Z_FIRST else (g_first, g_second, g_third)
        for i, f in zip((1, 2, 3), forms):
            steps[f"{name}{i}"] = lambda f=f, g=g: f(g)
    for name, g in (("a", a), ("b", b), ("k", k), ("l", l), ("m", m)):
        for i, what in enumerate(("one", "two", "other", "near", "far")):
            steps[f"w{name}{i + 1}"] = lambda g=g, what=what: last.insert(0, (last[0], getattr(g, what)))
    done = {}
    for name, g, which in (("a7", a, (0, 1)), ("b6", b, (0,)), ("b7", b, (1,))):
        steps[name] = lambda g=g, which=which: done.update(out=t_place(g, which, done.get("out")))
    steps["kl4"] = lambda: done.update(grad=g_final([k, l], done.get("grad")))
    steps["m4"] = lambda: done.update(grad=g_final([m], done.get("grad")))
    for step in ORDER:
        steps[step]()
    return (done["out"], done["grad"])


def solution(mesh):
    placed = (P("dp", None), P("dp", "tensor"), P("dp", "tensor"), P(None, "tensor"))
    return jax.shard_map(
        per_device,
        mesh=mesh,
        in_specs=placed,
        out_specs=(P("dp", None), P("dp", "tensor")),
        check_vma=False,
    )
```
